1024 devices in a mesh: row: 16 (over y_hi, z), col: 64 (over x, y_lo, core).
Axes of the slice: x: 8, y: 8 (y_hi: 2, y_lo: 4; y = y_hi * 4 + y_lo), z: 8, core: 2. Of those that a mesh axis runs over, the one named last changes fastest.
Arguments:
- inputs: bfloat16 [3, 128, 16384], P(None, 'col', 'row'), may hold values from -16 to 16
- weight: float32 [16384, 26624], P('row', 'col'), may hold values from -0.046875 to 0.046875
- upstream: bfloat16 [3, 128, 26624], P(None, 'row', 'col'), may hold values from -16 to 16
Outputs:
- activation: bfloat16 [3, 128, 26624], P(None, 'row', 'col')
- input_grad: bfloat16 [3, 128, 16384], P(None, 'col', 'row')
- weight_grad: float32 [16384, 26624], P('row', 'col')
The draws below stay inside these ranges and needn't reach their ends.
All inputs are finite; a program needn't handle non-finite values.
Results may differ from the reference program's by a relative error of at most 0.0063.
Values may be sent and summed in bfloat16 or wider, within the bound.
No kernel may reach another device: no remote copies, remote signals or barrier semaphores. Data moves between devices by JAX's collectives and lax.ppermute only.
A program may use at most 32 MiB of HBM per device.

```python
import math
import jax
import jax.numpy as jnp

D = 16384
F = 26624
MB_ROWS = 128
MICRO = 3


def raised(array, key, source, target, shards_of, factor):
    owner, partner = [(jnp.arange(array.shape[axis_at]) // (array.shape[axis_at] // shards_of)).reshape([-1 if axis == axis_at else 1 for axis in range(array.ndim)]) for axis_at in (source, target)]
    chosen = jax.random.permutation(key, shards_of)[partner]
    strong = (owner == chosen) | (owner == (partner + shards_of // 2) % shards_of)
    return jnp.where(strong, factor * array, array)


def level_of(stream_key, extent, pieces, smallest, top_value):
    def one(dim, parts):
        steps = jax.random.uniform(jax.random.fold_in(jax.random.fold_in(stream_key, 6), dim), (parts,), jnp.float32, smallest / len(pieces), top_value / len(pieces))
        return jnp.repeat(jnp.exp(steps), extent[dim] // parts).reshape((-1,) + (1,) * (len(extent) - dim - 1))

    gain = one(*pieces[0])
    for cut in pieces[1:]:
        gain = gain * one(*cut)
    return gain


def gaussian(own_key, dims, scale, limit, pieces=(), dtype=jnp.bfloat16):
    gain = level_of(own_key, dims, pieces, -0.22, 0.18) if pieces else 1.0
    drawn = jax.random.normal(own_key, dims, jnp.float32) * scale * gain
    return jnp.minimum(jnp.maximum(drawn, -limit), limit).astype(dtype)


def gaussian_with(own_key, shape, spread, bound, cuts, heavy, dtype=jnp.bfloat16):
    values = spread * jax.random.normal(own_key, shape, jnp.float32)
    if cuts:
        values = values * level_of(own_key, shape, cuts, -0.22, 0.18)
    return jnp.clip(raised(values, jax.random.fold_in(own_key, 3), *heavy), -bound, bound).astype(dtype)


def setup_inputs(seed: int = 0) -> dict:
    key_list = jax.random.split(jax.random.key(seed), 4)
    return {
        "inputs": gaussian_with(key_list[0], (MICRO, MB_ROWS, D), 1.0, 16.0, ((1, 64), (2, 16)), (2, 1, 64, 4.0)),
        "weight": gaussian(key_list[1], (D, F), D ** -0.5, 0.046875, ((0, 16), (1, 64)), jnp.float32),
        "upstream": gaussian_with(key_list[2], (MICRO, MB_ROWS, F), 1.0, 16.0, ((1, 16), (2, 64)), (2, 1, 64, 4.0)),
    }


def gelu_parts(pre):
    cdf = 0.5 * (1.0 + jax.scipy.special.erf(pre * (1.0 / math.sqrt(2.0))))
    slope = cdf + pre * jnp.exp(-0.5 * pre * pre) * (1.0 / math.sqrt(2.0 * math.pi))
    return (pre * cdf, slope)

def reference(inputs, weight, upstream):
    low = weight.astype(jnp.bfloat16)
    grad = jnp.zeros((D, F), jnp.float32)
    acts = []
    grads_in = []
    for index in range(MICRO):
        block = inputs[index]
        pre = jnp.dot(block, low, preferred_element_type=jnp.float32)
        act, slope = gelu_parts(pre)
        acts.append(act.astype(jnp.bfloat16))
        gated = (upstream[index].astype(jnp.float32) * slope).astype(jnp.bfloat16)
        grads_in.append(jnp.dot(gated, low.T, preferred_element_type=jnp.float32).astype(jnp.bfloat16))
        grad = grad + jnp.dot(block.T, gated, preferred_element_type=jnp.float32)
    grad = grad * (1.0 / math.sqrt(MICRO * MB_ROWS))
    return (jnp.stack(acts), jnp.stack(grads_in), grad)
```

```python
import math

import jax
import jax.numpy as jnp
from jax import lax
from jax.sharding import Mesh, PartitionSpec as P

BF = jnp.bfloat16
F32 = jnp.float32
SWAP = [(0, 1), (1, 0)]


def gelu_parts(pre):
    cdf = 0.5 * (1.0 + jax.scipy.special.erf(pre * (1.0 / math.sqrt(2.0))))
    slope = cdf + pre * jnp.exp(-0.5 * pre * pre) * (1.0 / math.sqrt(2.0 * math.pi))
    return (pre * cdf, slope)


def copy_for_each(shard, axis):
    copies = jnp.broadcast_to(shard, (lax.axis_size(axis), *shard.shape))
    return lax.all_to_all(copies, axis, split_axis=0, concat_axis=0, tiled=True)


def exchange(pieces, axis):
    return lax.all_to_all(pieces, axis, split_axis=0, concat_axis=0, tiled=True)


def body(inputs, weight, upstream):
    micro, own, width = inputs.shape
    hidden = weight.shape[1]
    rows, chips = lax.axis_size("row"), lax.axis_size("chip")
    tokens = upstream.shape[1]
    me = lax.axis_index("core")
    total = chips * micro * own
    mine = total // rows
    spare = -(2 * hidden) % 128

    low = weight.T.astype(BF)
    split = upstream.reshape(micro, tokens // (2 * own), 2, own, hidden)
    split = jnp.moveaxis(split, 2, 0).transpose(0, 2, 1, 3, 4).reshape(2, mine, hidden)
    kept = lax.dynamic_index_in_dim(split, me, 0, keepdims=False)
    given = lax.dynamic_index_in_dim(split, 1 - me, 0, keepdims=False)
    other_low = lax.ppermute(low, "core", SWAP)
    other_up = lax.ppermute(given, "core", SWAP)
    both = jnp.concatenate([low, other_low, jnp.zeros((spare, width), BF)], 0)
    up = jnp.concatenate([kept, other_up, jnp.zeros((mine, spare), BF)], 1)

    x = copy_for_each(inputs, "chip").reshape(total, width)
    part = lax.dot_general(x, both, (((1,), (1,)), ((), ())), preferred_element_type=F32)
    part = part.astype(BF).reshape(rows, mine // 4, 4, -1)
    pieces = exchange(part, "row").reshape(rows, mine, -1)
    other_x = lax.ppermute(x, "core", SWAP)

    act, slope = gelu_parts(jnp.sum(pieces.astype(F32), axis=0))
    gated = (up.astype(F32) * slope).astype(BF)
    act = act.astype(BF)
    gathered = copy_for_each(gated.reshape(mine // 4, 4, -1), "row").reshape(total, -1)

    term = lax.dot_general(gathered, both, (((1,), (0,)), ((), ())), preferred_element_type=F32)
    dx = exchange(term.astype(BF).reshape(chips, micro, own, width), "chip")

    other_gated = lax.ppermute(gathered[:, hidden : 2 * hidden], "core", SWAP)
    other_act = lax.ppermute(act[:, hidden : 2 * hidden], "core", SWAP)
    xs = jnp.concatenate([x, other_x], 0)
    gs = jnp.concatenate([gathered[:, :hidden], other_gated], 0)
    grad = lax.dot_general(xs, gs, (((0,), (0,)), ((), ())), preferred_element_type=F32)
    grad = grad * (1.0 / math.sqrt(2 * total))

    shape = (tokens // (2 * own), micro, own, hidden)
    held, got = act[:, :hidden].reshape(shape), other_act.reshape(shape)
    acts = jnp.stack([jnp.where(me == 0, held, got), jnp.where(me == 0, got, held)], 2)
    acts = jnp.moveaxis(acts, 0, 1).reshape(micro, tokens, hidden)
    input_grad = jnp.sum(dx.astype(F32), axis=0).astype(BF)
    return (acts, input_grad, grad)


def solution(mesh):
    rows, cols = mesh.devices.shape
    fine = Mesh(mesh.devices.reshape(rows, cols // 2, 2), ("row", "chip", "core"))
    col = ("chip", "core")
    placed = (P(None, col, "row"), P("row", col), P(None, "row", col))
    return jax.shard_map(
        body,
        mesh=fine,
        in_specs=placed,
        out_specs=(P(None, "row", col), P(None, col, "row"), P("row", col)),
        check_vma=False,
    )
```

```python
import math

import jax
import jax.numpy as jnp
from jax import lax
from jax.sharding import Mesh, PartitionSpec as P


BF = jnp.bfloat16
F32 = jnp.float32
SWAP = [(0, 1), (1, 0)]
AXES = ("yh", "z", "xh", "xl", "y1", "y0", "core")
ROW = ("yh", "z")
COL = ("xh", "xl", "y1", "y0", "core")
CHIP = ("xl", "y1", "xh", "y0")


def exchange(pieces, axis):
    return lax.all_to_all(pieces, axis, split_axis=0, concat_axis=0, tiled=True)


def copy_for_each(shard, axis):
    return exchange(jnp.broadcast_to(shard, (lax.axis_size(axis), *shard.shape)), axis)


def swapped(value, axis="core"):
    return lax.ppermute(value, axis, SWAP)


def body(inputs, weight, upstream):
    micro, own, width = inputs.shape
    hidden = weight.shape[1]
    depth, chips = lax.axis_size("z"), lax.axis_size(CHIP)
    tokens = upstream.shape[1]
    core, half = lax.axis_index("core"), lax.axis_index("yh")
    total = chips * micro * own
    mine = total // (2 * depth)
    spare = -(2 * hidden) % 128

    x = copy_for_each(inputs, CHIP)
    x = x.reshape(total, width)

    low = weight.T.astype(BF)
    both = jnp.concatenate([low, swapped(low), jnp.zeros((spare, width), BF)], 0)
    split = upstream.reshape(micro, tokens // (2 * own), 2, own, hidden)
    split = split.transpose(2, 1, 0, 3, 4).reshape(2, mine, hidden)
    kept = jnp.where(core == 0, split[0], split[1])
    given = jnp.where(core == 0, split[1], split[0])
    up = jnp.concatenate([kept, swapped(given), jnp.zeros((mine, spare), BF)], 1)
    far = swapped(up, "yh")
    up = jnp.concatenate([jnp.where(half == 0, up, far), jnp.where(half == 0, far, up)], 0)

    part = lax.dot_general(x, both, (((1,), (1,)), ((), ())), preferred_element_type=F32)
    pieces = exchange(part.astype(BF).reshape(depth, 2 * mine, -1), "z")
    partial = jnp.sum(pieces.astype(F32), axis=0).astype(BF)
    other = swapped(partial, "yh")
    other_x = swapped(x)
    pre = partial.astype(F32) + other.astype(F32)

    cdf = 0.5 * (1.0 + jax.scipy.special.erf(pre * (1.0 / math.sqrt(2.0))))
    slope = cdf + pre * jnp.exp(-0.5 * pre * pre) * (1.0 / math.sqrt(2.0 * math.pi))
    gated = (up.astype(F32) * slope).astype(BF)
    gathered = copy_for_each(gated, "z").reshape(total, -1)

    term = lax.dot_general(gathered, both, (((1,), (0,)), ((), ())), preferred_element_type=F32)
    dx = exchange(term.astype(BF).reshape(chips, micro, own, width), CHIP)
    act = pre * cdf
    act = jnp.where(half == 0, act[:mine], act[mine:]).astype(BF)
    other_act = swapped(act[:, hidden : 2 * hidden])

    other_gated = swapped(gathered[:, hidden : 2 * hidden])
    xs = jnp.concatenate([x, other_x], 0)
    gs = jnp.concatenate([gathered[:, :hidden], other_gated], 0)
    grad = lax.dot_general(xs, gs, (((0,), (0,)), ((), ())), preferred_element_type=F32)
    grad = grad * (1.0 / math.sqrt(2 * total))

    shape = (tokens // (2 * own), micro, own, hidden)
    held, got = act[:, :hidden].reshape(shape), other_act.reshape(shape)
    acts = jnp.stack([jnp.where(core == 0, held, got), jnp.where(core == 0, got, held)], 2)
    acts = jnp.moveaxis(acts, 0, 1).reshape(micro, tokens, hidden)
    input_grad = jnp.sum(dx.astype(F32), axis=0).astype(BF)
    return (acts, input_grad, grad)


def solution(mesh):
    fine = Mesh(mesh.devices.reshape(2, 8, 2, 4, 2, 2, 2), AXES)
    return jax.shard_map(
        body,
        mesh=fine,
        in_specs=(P(None, COL, ROW), P(ROW, COL), P(None, ROW, COL)),
        out_specs=(P(None, ROW, COL), P(None, COL, ROW), P(ROW, COL)),
        check_vma=False,
    )
```

```python
import math

import jax
import jax.numpy as jnp
from jax import lax
from jax.sharding import Mesh, PartitionSpec as P


BF = jnp.bfloat16
F32 = jnp.float32
SWAP = [(0, 1), (1, 0)]
AXES = ("yh", "z", "xh", "xl", "y1", "y0", "core")
ROW = ("yh", "z")
COL = ("xh", "xl", "y1", "y0", "core")
CHIP = ("xl", "y1", "xh", "y0")


def exchange(pieces, axis):
    return lax.all_to_all(pieces, axis, split_axis=0, concat_axis=0, tiled=True)


def copy_for_each(shard, axis):
    return exchange(jnp.broadcast_to(shard, (lax.axis_size(axis), *shard.shape)), axis)


def swapped(value, axis="core"):
    return lax.ppermute(value, axis, SWAP)


def body(inputs, weight, upstream):
    micro, own, width = inputs.shape
    hidden = weight.shape[1]
    depth, chips = lax.axis_size("z"), lax.axis_size(CHIP)
    tokens = upstream.shape[1]
    core, half = lax.axis_index("core"), lax.axis_index("yh")
    total = chips * micro * own
    mine = total // (2 * depth)
    spare = -(2 * hidden) % 128

    x = copy_for_each(inputs, CHIP)
    x = x.reshape(total, width)

    low = weight.T.astype(BF)
    other_low = swapped(low)
    both = jnp.concatenate([low, other_low, jnp.zeros((spare, width), BF)], 0)
    both = lax.optimization_barrier(both)
    split = upstream.reshape(micro, tokens // (2 * own), 2, own, hidden)
    split = split.transpose(2, 1, 0, 3, 4).reshape(2, mine, hidden)
    kept = jnp.where(core == 0, split[0], split[1])
    given = jnp.where(core == 0, split[1], split[0])
    up = jnp.concatenate([kept, swapped(given), jnp.zeros((mine, spare), BF)], 1)

    part = lax.dot_general(x, both, (((1,), (1,)), ((), ())), preferred_element_type=F32)
    pieces = exchange(part.astype(BF).reshape(depth, 2 * mine, -1), "z")
    other_x = swapped(x)
    partial = jnp.sum(pieces.astype(F32), axis=0).astype(BF)
    other = swapped(jnp.concatenate([partial, up], 0), "yh")
    far = other[2 * mine :]
    pre = partial.astype(F32) + other[: 2 * mine].astype(F32)
    up = jnp.concatenate([jnp.where(half == 0, up, far), jnp.where(half == 0, far, up)], 0)

    cdf = 0.5 * (1.0 + jax.scipy.special.erf(pre * (1.0 / math.sqrt(2.0))))
    slope = cdf + pre * jnp.exp(-0.5 * pre * pre) * (1.0 / math.sqrt(2.0 * math.pi))
    gated = (up.astype(F32) * slope).astype(BF)
    gathered = copy_for_each(gated, "z").reshape(total, -1)

    term = lax.dot_general(gathered, both, (((1,), (0,)), ((), ())), preferred_element_type=F32)
    dx = exchange(term.astype(BF).reshape(chips, micro, own, width), CHIP)
    act = pre * cdf
    act = jnp.where(half == 0, act[:mine], act[mine:]).astype(BF)
    other_act = swapped(act[:, hidden : 2 * hidden])

    other_gated = swapped(gathered[:, hidden : 2 * hidden])
    xs = jnp.concatenate([x, other_x], 0)
    gs = jnp.concatenate([gathered[:, :hidden], other_gated], 0)
    grad = lax.dot_general(xs, gs, (((0,), (0,)), ((), ())), preferred_element_type=F32)
    grad = grad * (1.0 / math.sqrt(2 * total))

    shape = (tokens // (2 * own), micro, own, hidden)
    held, got = act[:, :hidden].reshape(shape), other_act.reshape(shape)
    acts = jnp.stack([jnp.where(core == 0, held, got), jnp.where(core == 0, got, held)], 2)
    acts = jnp.moveaxis(acts, 0, 1).reshape(micro, tokens, hidden)
    input_grad = jnp.sum(dx.astype(F32), axis=0).astype(BF)
    return (acts, input_grad, grad)


def solution(mesh):
    fine = Mesh(mesh.devices.reshape(2, 8, 2, 4, 2, 2, 2), AXES)
    return jax.shard_map(
        body,
        mesh=fine,
        in_specs=(P(None, COL, ROW), P(ROW, COL), P(None, ROW, COL)),
        out_specs=(P(None, ROW, COL), P(None, COL, ROW), P(ROW, COL)),
        check_vma=False,
    )
```

```python
import math

import jax
import jax.numpy as jnp
from jax import lax
from jax.sharding import Mesh, PartitionSpec as P


BF = jnp.bfloat16
F32 = jnp.float32
SWAP = [(0, 1), (1, 0)]
AXES = ("yh", "z", "xh", "xl", "y1", "y0", "core")
ROW = ("yh", "z")
COL = ("xh", "xl", "y1", "y0", "core")
CHIP = ("xl", "y1", "xh", "y0")


def exchange(pieces, axis):
    return lax.all_to_all(pieces, axis, split_axis=0, concat_axis=0, tiled=True)


def copy_for_each(shard, axis):
    return exchange(jnp.broadcast_to(shard, (lax.axis_size(axis), *shard.shape)), axis)


def swapped(value, axis="core"):
    return lax.ppermute(value, axis, SWAP)


def body(inputs, weight, upstream):
    micro, own, width = inputs.shape
    hidden = weight.shape[1]
    depth, chips = lax.axis_size("z"), lax.axis_size(CHIP)
    tokens = upstream.shape[1]
    core, half = lax.axis_index("core"), lax.axis_index("yh")
    total = chips * micro * own
    mine = total // (2 * depth)
    spare = -(2 * hidden) % 128

    x = copy_for_each(inputs, CHIP)
    x = x.reshape(total, width)

    low = weight.T.astype(BF)
    other_low = swapped(low)
    both = jnp.concatenate([low, other_low, jnp.zeros((spare, width), BF)], 0)
    both = lax.optimization_barrier(both)
    split = upstream.reshape(micro, tokens // (2 * own), 2, own, hidden)
    split = split.transpose(2, 1, 0, 3, 4).reshape(2, mine, hidden)
    kept = jnp.where(core == 0, split[0], split[1])
    given = jnp.where(core == 0, split[1], split[0])
    up = jnp.concatenate([kept, swapped(given), jnp.zeros((mine, spare), BF)], 1)

    part = lax.dot_general(x, both, (((1,), (1,)), ((), ())), preferred_element_type=F32)
    pieces = exchange(part.astype(BF).reshape(depth, 2 * mine, -1), "z")
    partial = jnp.sum(pieces.astype(F32), axis=0).astype(BF)
    other = swapped(jnp.concatenate([partial, up], 0), "yh")
    other_x = swapped(x)
    first = half == 0
    far = other[2 * mine :]
    pre = partial.astype(F32) + other[: 2 * mine].astype(F32)
    up = jnp.concatenate([jnp.where(first, up, far), jnp.where(first, far, up)], 0)

    cdf = 0.5 * (1.0 + jax.scipy.special.erf(pre * (1.0 / math.sqrt(2.0))))
    slope = cdf + pre * jnp.exp(-0.5 * pre * pre) * (1.0 / math.sqrt(2.0 * math.pi))
    gated = (up.astype(F32) * slope).astype(BF)
    gathered = copy_for_each(gated, "z").reshape(total, -1)

    term = lax.dot_general(gathered, both, (((1,), (0,)), ((), ())), preferred_element_type=F32)
    dx = exchange(term.astype(BF).reshape(chips, micro, own, width), CHIP)
    act = pre * cdf
    act = jnp.where(first, act[:mine], act[mine:]).astype(BF)
    other_act = swapped(act[:, hidden : 2 * hidden])

    other_gated = swapped(gathered[:, hidden : 2 * hidden])
    xs = jnp.concatenate([x, other_x], 0)
    gs = jnp.concatenate([gathered[:, :hidden], other_gated], 0)
    grad = lax.dot_general(xs, gs, (((0,), (0,)), ((), ())), preferred_element_type=F32)
    grad = grad * (1.0 / math.sqrt(2 * total))

    shape = (tokens // (2 * own), micro, own, hidden)
    held, got = act[:, :hidden].reshape(shape), other_act.reshape(shape)
    acts = jnp.stack([jnp.where(core == 0, held, got), jnp.where(core == 0, got, held)], 2)
    acts = jnp.moveaxis(acts, 0, 1).reshape(micro, tokens, hidden)
    input_grad = jnp.sum(dx.astype(F32), axis=0).astype(BF)
    return (acts, input_grad, grad)


def solution(mesh):
    fine = Mesh(mesh.devices.reshape(2, 8, 2, 4, 2, 2, 2), AXES)
    return jax.shard_map(
        body,
        mesh=fine,
        in_specs=(P(None, COL, ROW), P(ROW, COL), P(None, ROW, COL)),
        out_specs=(P(None, ROW, COL), P(None, COL, ROW), P(ROW, COL)),
        check_vma=False,
    )
```
